32 devices in a mesh: band: 4 (over x, core), freq: 8 (over z, y).
Axes of the slice: x: 2, y: 2, z: 4, core: 2. Of those that a mesh axis runs over, the one named last changes fastest.
Arguments:
- samples: float32 [2048, 16384], P('band', 'freq'), may hold values from -6 to 6
- channel_delay: int32 [2048, 64], P('band'), may hold values from 0 to 4095
- merge_slope: int32 [7], replicated, may hold values from 16 to 1023
- tap_offset: int32 [32, 16], replicated, may hold values from -32 to 32, as said below
- tap_weight: float32 [32, 16], replicated, may hold values from -1.5 to 1.5
Outputs:
- best_power: float32 [512, 8192], P('band', 'freq')
The draws below stay inside these ranges and needn't reach their ends.
Inputs may be any that keep to these rules, and one draw needn't show every extreme that they name: `tap_offset`: in every draw some template has a tap at offset -32 and some template has one at 32.
All inputs are finite; a program needn't handle non-finite values.
Results may differ from the reference program's by a relative error of at most 0.0003.
Values sent between devices are 32-bit elements; how exact they have to be, the bound alone decides.
A program may use at most 256 MiB of HBM per device.

```python
import math
import jax
import jax.numpy as jnp
import numpy as np
from jax import lax

CH_SUB = 256
SAMPLES = 16384
SUB_DELAYS = 64
TEMPLATES = 32
TAPS = 16
REACH = 32
SUBBANDS = 8
CHANNELS = 2048
HALF = 8192
FINAL = 512


def draw_tap_offset(key, part):
    key_table = jax.random.fold_in(key, 11)
    key_pick = jax.random.fold_in(key, 12)
    offsets_table = jax.random.randint(key_table, (TEMPLATES, TAPS), -REACH, REACH + 1)
    chosen = jax.random.randint(key_pick, (2,), 0, TEMPLATES)
    offsets_table = offsets_table.at[chosen[0], 0].set(-REACH)
    offsets_table = offsets_table.at[chosen[1], 1].set(REACH)
    return offsets_table.astype(jnp.int32)


def set_ends(values, own_key, smallest, top_value):
    place = [jax.random.randint(jax.random.fold_in(own_key, axis), (), 0, length) for axis, length in enumerate(values.shape)]
    longest = values.shape.index(max(values.shape))
    next_to = place[:longest] + [(place[longest] + 1) % values.shape[longest]] + place[longest + 1:]
    return values.at[tuple(place)].set(smallest).at[tuple(next_to)].set(top_value)


def block_scale(own_key, dims, pieces, low, top_value):
    factor_of, own = 1.0, jax.random.fold_in(own_key, 6)
    for axis_at, shards_of in pieces:
        steps = jnp.exp(jax.random.uniform(jax.random.fold_in(own, axis_at), (shards_of,), jnp.float32, low / len(pieces), top_value / len(pieces)))
        factor_of = factor_of * jnp.repeat(steps, dims[axis_at] // shards_of).reshape([-1 if axis == axis_at else 1 for axis in range(len(dims))])
    return factor_of


def centred(key, dims, scale, reach, shards=(), held_as=jnp.bfloat16):
    factor_of = block_scale(key, dims, shards, -0.22, 0.18) if shards else 1.0
    drawn = jax.random.normal(key, dims, jnp.float32) * scale * factor_of
    return jnp.minimum(jnp.maximum(drawn, -reach), reach).astype(held_as)


def setup_inputs(seed: int = 0) -> dict:
    keys = jax.random.split(jax.random.key(seed), 6)
    samples = centred(keys[0], (CHANNELS, SAMPLES), 1.0, 6.0, ((0, 4), (1, 8)), jnp.float32)
    channel_delay = set_ends(jax.random.randint(keys[1], (CHANNELS, SUB_DELAYS), 0, 4096), jax.random.fold_in(keys[1], 1), 0, 4095).astype(jnp.int32)
    merge_slope = set_ends(jax.random.randint(keys[2], (SUBBANDS - 1,), 16, 1024), jax.random.fold_in(keys[2], 1), 16, 1023).astype(jnp.int32)
    tap_offset = draw_tap_offset(jax.random.fold_in(keys[5], 71), 0)
    tap_weight = centred(keys[4], (TEMPLATES, TAPS), TAPS ** -0.5, 1.5, (), jnp.float32)
    return {"samples": samples, "channel_delay": channel_delay, "merge_slope": merge_slope, "tap_offset": tap_offset, "tap_weight": tap_weight}


two_pi = 2.0 * math.pi

def turning(count, modulus):
    angle = (count % modulus).astype(jnp.float32) * (two_pi / modulus)
    return (jnp.cos(angle), jnp.sin(angle))

def rotate(real, imag, cosine, sine_part):
    return (real * cosine + imag * sine_part, imag * cosine - real * sine_part)

def merge_nodes(lower_half, upper_half, out_index, slopes, bins_index, modulus):
    shift = out_index[None, :] * slopes[:, None] // 16 % modulus
    cosine, sine_part = turning(shift[:, :, None] * bins_index[None, None, :], modulus)
    up_re, up_im = rotate(upper_half[0], upper_half[1], cosine, sine_part)
    return jnp.stack([lower_half[0] + up_re, lower_half[1] + up_im]) * (1.0 / math.sqrt(2.0))

def reference(samples, channel_delay, merge_slope, tap_offset, tap_weight):
    spectrum = jnp.fft.rfft(samples, axis=1)[:, :HALF] / math.sqrt(SAMPLES)
    spec_re = jnp.real(spectrum).astype(jnp.float32)
    spec_im = jnp.imag(spectrum).astype(jnp.float32)
    fine_bins = lax.iota(jnp.int32, 128)
    coarse_bins = lax.iota(jnp.int32, HALF // 128) * 128

    def one_subband(inputs):
        band_re, band_im, band_delay = inputs
        delay_blocks = band_delay.reshape(CH_SUB, SUB_DELAYS // 8, 8).transpose(1, 0, 2)

        def one_block(delay_cols):
            coarse_cos, coarse_sin = turning(delay_cols[:, :, None] * coarse_bins[None, None, :], SAMPLES)
            fine_cos, fine_sin = turning(delay_cols[:, :, None] * fine_bins[None, None, :], SAMPLES)
            full_cos = coarse_cos[..., None] * fine_cos[..., None, :] - coarse_sin[..., None] * fine_sin[..., None, :]
            full_sin = coarse_sin[..., None] * fine_cos[..., None, :] + coarse_cos[..., None] * fine_sin[..., None, :]
            full_cos = full_cos.reshape(CH_SUB, 8, HALF)
            full_sin = full_sin.reshape(CH_SUB, 8, HALF)
            turned_re, turned_im = rotate(band_re[:, None, :], band_im[:, None, :], full_cos, full_sin)
            return (lax.optimization_barrier(jnp.sum(turned_re, axis=0)), lax.optimization_barrier(jnp.sum(turned_im, axis=0)))
        sums_re, sums_im = lax.map(one_block, delay_blocks)
        return (sums_re.reshape(SUB_DELAYS, HALF), sums_im.reshape(SUB_DELAYS, HALF))
    sub_re, sub_im = lax.map(one_subband, (spec_re.reshape(SUBBANDS, CH_SUB, HALF), spec_im.reshape(SUBBANDS, CH_SUB, HALF), channel_delay.reshape(SUBBANDS, CH_SUB, SUB_DELAYS)))
    current = jnp.stack([sub_re, sub_im]) * (1.0 / math.sqrt(CH_SUB))
    bins_index = lax.iota(jnp.int32, HALF)
    section_count = SUBBANDS.bit_length() - 1
    for section_no in range(section_count):
        d_in = current.shape[2]
        lower_half = current[:, 0::2]
        upper_half = current[:, 1::2]
        lower_half = jnp.concatenate([lower_half, lower_half], axis=2)
        upper_half = jnp.concatenate([upper_half, upper_half], axis=2)
        node_count = lower_half.shape[1]
        slope_rows = merge_slope[np.array([node_no * (2 << section_no) + (1 << section_no) - 1 for node_no in range(node_count)], dtype=np.int32)]
        current = merge_nodes(lower_half, upper_half, lax.iota(jnp.int32, 2 * d_in), slope_rows, bins_index, SAMPLES)
    padded_re = jnp.pad(current[0, 0], ((0, 0), (REACH, REACH)))
    padded_im = jnp.pad(current[1, 0], ((0, 0), (REACH, REACH)))

    def one_template(template_no, best):

        def one_tap(tap_no, totals):
            start = (tap_offset[template_no, tap_no] + REACH).astype(jnp.int32)
            weight = tap_weight[template_no, tap_no]
            return (totals[0] + weight * lax.dynamic_slice_in_dim(padded_re, start, HALF, 1), totals[1] + weight * lax.dynamic_slice_in_dim(padded_im, start, HALF, 1))
        zeros_grid = jnp.zeros((FINAL, HALF), jnp.float32)
        corr_re, corr_im = lax.fori_loop(0, TAPS, one_tap, (zeros_grid, zeros_grid))
        return jnp.maximum(best, corr_re * corr_re + corr_im * corr_im)
    return lax.fori_loop(0, TEMPLATES, one_template, jnp.zeros((FINAL, HALF), jnp.float32))
```

```python
import functools
import math

import jax
import jax.numpy as jnp
import numpy as np
from jax import lax
from jax.experimental import pallas as pl
from jax.experimental.pallas import tpu as pltpu
from jax.sharding import PartitionSpec as P

REACH = 32
DELAY_BOUND = 4096
LANES = 128
GROUP = 8


two_pi = 2.0 * math.pi


def from_partner(value, axis, stride):
    return lax.ppermute(value, axis, [(i, i ^ 1 << stride) for i in range(lax.axis_size(axis))])


def extended(cells, sides, width):
    for axis, dim in sides:
        count = lax.axis_size(axis)
        ends = count - 1
        head = lax.slice_in_dim(cells, 0, width, axis=dim)
        tail = lax.slice_in_dim(cells, cells.shape[dim] - width, cells.shape[dim], axis=dim)
        cells = jnp.concatenate(
            [
                lax.ppermute(tail, axis, [(i, (i + 1) % count) for i in range(ends)]),
                cells,
                lax.ppermute(head, axis, [((i + 1) % count, i) for i in range(ends)]),
            ],
            axis=dim,
        )
    return cells


def turning(count, modulus):
    angle = (count % modulus).astype(jnp.float32) * (two_pi / modulus)
    return (jnp.cos(angle), jnp.sin(angle))


def rotate(real, imag, cosine, sine_part):
    return (real * cosine + imag * sine_part, imag * cosine - real * sine_part)


def merge_nodes(lower_half, upper_half, out_index, slopes, bins_index, modulus):
    shift = out_index[None, :] * slopes[:, None] // 16 % modulus
    cosine, sine_part = turning(shift[:, :, None] * bins_index[None, None, :], modulus)
    up_re, up_im = rotate(upper_half[0], upper_half[1], cosine, sine_part)
    return jnp.stack([lower_half[0] + up_re, lower_half[1] + up_im]) * (1.0 / math.sqrt(2.0))


def pick_entry(table, index):
    return jnp.sum(jnp.where(lax.iota(jnp.int32, table.shape[0]) == index, table, 0))


def shift_sum_kernel(delay_ref, series_ref, out_ref, rows_ref, window_ref):
    step = pl.program_id(0)
    parts, _, part_len = series_ref.shape
    outer = part_len // LANES
    count = parts * outer
    turns = DELAY_BOUND // LANES
    for part in range(parts):
        for block in range(outer):
            rows_ref[pl.ds((part * outer + block) * GROUP, GROUP), :] = series_ref[
                part, :, block * LANES : (block + 1) * LANES
            ]

    for chan in range(GROUP):
        grid = rows_ref[pl.ds(chan, count, stride=GROUP), :].T
        for turn in range(turns + 1):
            shift = (turns - turn) % count
            window_ref[chan, turn * LANES : (turn + 1) * LANES, :] = (
                pltpu.roll(grid, shift, 1) if shift else grid
            )

    @pl.when(step == 0)
    def _():
        out_ref[...] = jnp.zeros_like(out_ref)

    def one_delay(delay_no, carry):
        total = out_ref[delay_no]
        for chan in range(GROUP):
            start = DELAY_BOUND - delay_ref[step * GROUP + chan, delay_no]
            total = total + window_ref[chan, pl.ds(start, LANES), :]
        out_ref[delay_no] = total
        return carry

    lax.fori_loop(0, out_ref.shape[0], one_delay, 0)


def shift_sum(delays, series):
    parts, chan_count, part_len = series.shape
    delay_count = delays.shape[1]
    count = parts * part_len // LANES
    return pl.pallas_call(
        shift_sum_kernel,
        out_shape=jax.ShapeDtypeStruct((delay_count, LANES, count), jnp.float32),
        grid_spec=pltpu.PrefetchScalarGridSpec(
            num_scalar_prefetch=1,
            grid=(chan_count // GROUP,),
            in_specs=[pl.BlockSpec((parts, GROUP, part_len), lambda i, _: (0, i, 0))],
            out_specs=pl.BlockSpec((delay_count, LANES, count), lambda i, _: (0, 0, 0)),
            scratch_shapes=[
                pltpu.VMEM((count * GROUP, LANES), jnp.float32),
                pltpu.VMEM((GROUP, DELAY_BOUND + LANES, count), jnp.float32),
            ],
        ),
        compiler_params=pltpu.CompilerParams(vmem_limit_bytes=48 << 20),
        name="shift_sum",
    )(delays, series)


def dft_kernel(first_ref, twist_cos_ref, twist_sin_ref, second_ref, parts_ref, out_ref):
    grid = parts_ref[0, 0]
    for part in range(1, parts_ref.shape[0]):
        grid = grid + parts_ref[part, 0]
    count = grid.shape[1]
    top = lax.Precision.HIGHEST
    part_out = jnp.dot(grid, first_ref[...], precision=top, preferred_element_type=jnp.float32)
    real, imag = rotate(
        part_out[:, :count], part_out[:, count:], twist_cos_ref[...], twist_sin_ref[...]
    )
    both = jnp.concatenate([real, imag], axis=0)
    spectrum = jnp.dot(second_ref[...], both, precision=top, preferred_element_type=jnp.float32)
    slabs, _, _, rows, _ = out_ref.shape
    half = slabs * rows
    for slab in range(slabs):
        out_ref[slab, 0, 0] = spectrum[slab * rows : (slab + 1) * rows]
        out_ref[slab, 1, 0] = spectrum[half + slab * rows : half + (slab + 1) * rows]


def dft(parts, slabs, scale):
    part_count, row_count, inner, outer = parts.shape
    length = inner * outer
    kept = inner // 2
    rows = kept // slabs
    index = np.arange(outer)
    angle = (index[:, None] * index[None, :] % outer) * (two_pi / outer)
    first = np.concatenate([np.cos(angle), -np.sin(angle)], axis=1)
    angle = (np.arange(inner)[:, None] * index[None, :]) * (two_pi / length)
    twist_cos, twist_sin = np.cos(angle), np.sin(angle)
    angle = (np.arange(kept)[:, None] * np.arange(inner)[None, :] % inner) * (two_pi / inner)
    cosine, sine_part = np.cos(angle) * scale, np.sin(angle) * scale
    second = np.block([[cosine, sine_part], [-sine_part, cosine]])
    tables = [jnp.asarray(t, jnp.float32) for t in (first, twist_cos, twist_sin, second)]
    whole = [pl.BlockSpec(t.shape, lambda i: (0, 0)) for t in tables]
    return pl.pallas_call(
        dft_kernel,
        out_shape=jax.ShapeDtypeStruct((slabs, 2, row_count, rows, outer), jnp.float32),
        grid=(row_count,),
        in_specs=whole
        + [pl.BlockSpec((part_count, 1, inner, outer), lambda i: (0, i, 0, 0))],
        out_specs=pl.BlockSpec((slabs, 2, 1, rows, outer), lambda i: (0, 0, i, 0, 0)),
        name="dft",
    )(*tables, parts)


def split_halves(value):
    coarse = value.astype(jnp.bfloat16)
    fine = (value - coarse.astype(jnp.float32)).astype(jnp.bfloat16)
    return coarse, fine


def template_kernel(profile_ref, left_ref, right_ref, out_ref, bank_ref):
    template_count, width = profile_ref.shape

    @pl.when(pl.program_id(0) == 0)
    def _():
        def one_template(template_no, carry):
            row = jnp.broadcast_to(profile_ref[pl.ds(template_no, 1), :], (LANES, width))
            coarse, fine = split_halves(pltpu.roll(row, 0, 1, stride=1, stride_axis=0))
            where = pl.ds(pl.multiple_of(template_no * LANES, LANES), LANES)
            bank_ref[where, :] = jnp.concatenate([coarse, coarse, fine], axis=1)
            return carry

        lax.fori_loop(0, template_count, one_template, 0)

    coarse, fine = split_halves(jnp.concatenate([left_ref[...], right_ref[...]], axis=1))
    cells = jnp.concatenate([coarse, fine, coarse], axis=1)
    rows = out_ref.shape[0]
    best = jnp.zeros_like(out_ref)
    for pair in range(template_count // 2):
        corr = lax.dot_general(
            cells,
            bank_ref[pair * 2 * LANES : (pair + 1) * 2 * LANES, :],
            (((1,), (1,)), ((), ())),
            preferred_element_type=jnp.float32,
        )
        power = corr[:rows] * corr[:rows] + corr[rows:] * corr[rows:]
        best = jnp.maximum(best, jnp.maximum(power[:, :LANES], power[:, LANES:]))
    out_ref[...] = best


def template_search(profile, cells, bins_dev):
    rows = cells.shape[0] // 2
    template_count, width = profile.shape
    return pl.pallas_call(
        template_kernel,
        out_shape=jax.ShapeDtypeStruct((rows, bins_dev), jnp.float32),
        grid=(bins_dev // LANES,),
        in_specs=[
            pl.BlockSpec((template_count, width), lambda i: (0, 0)),
            pl.BlockSpec((2 * rows, LANES), lambda i: (0, i)),
            pl.BlockSpec((2 * rows, LANES), lambda i: (0, i + 1)),
        ],
        out_specs=pl.BlockSpec((rows, LANES), lambda i: (0, i)),
        scratch_shapes=[pltpu.VMEM((template_count * LANES, 3 * width), jnp.bfloat16)],
        compiler_params=pltpu.CompilerParams(vmem_limit_bytes=48 << 20),
        name="template_search",
    )(profile, cells, cells)


def per_device(samples, channel_delay, merge_slope, tap_offset, tap_weight):
    freq_count = lax.axis_size("freq")
    band_count = lax.axis_size("band")
    band_pos = lax.axis_index("band")
    freq_pos = lax.axis_index("freq")
    chan_dev, samp_dev = samples.shape
    length = samp_dev * freq_count
    bins_dev = length // 2 // freq_count
    delays_sub = channel_delay.shape[1]
    block_rows = 2 * delays_sub
    per_sub = chan_dev // 2
    chan_own = chan_dev // freq_count
    share = per_sub // chan_own
    bins_index = freq_pos * bins_dev + lax.iota(jnp.int32, bins_dev)

    series = lax.all_to_all(
        samples.reshape(freq_count, chan_own, samp_dev), "freq", split_axis=0, concat_axis=0, tiled=True
    )
    own_delay = lax.dynamic_slice_in_dim(channel_delay, freq_pos * chan_own, chan_own, axis=0)
    partial = shift_sum(own_delay, series)
    inner, outer = partial.shape[1:]
    groups = [list(range(g * share, (g + 1) * share)) for g in range(freq_count // share)]
    parts = lax.all_to_all(
        partial.reshape(share, delays_sub // share, inner, outer),
        "freq", split_axis=0, concat_axis=0, axis_index_groups=groups, tiled=True,
    )
    slabs = dft(parts, freq_count, 1.0 / math.sqrt(length * per_sub))
    slabs = lax.all_to_all(slabs, "freq", split_axis=0, concat_axis=0, tiled=True)
    subband_sums = (
        slabs.reshape(2, share, 2, delays_sub // share, bins_dev)
        .transpose(2, 0, 1, 3, 4)
        .reshape(2, 2, delays_sub, bins_dev)
    )
    lower_half = jnp.concatenate([subband_sums[:, 0:1], subband_sums[:, 0:1]], axis=2)
    upper_half = jnp.concatenate([subband_sums[:, 1:2], subband_sums[:, 1:2]], axis=2)
    first_slope = pick_entry(merge_slope, 2 * band_pos).reshape(1)
    level_zero = merge_nodes(
        lower_half, upper_half, lax.iota(jnp.int32, block_rows), first_slope, bins_index, length
    )
    section_count = band_count.bit_length() - 1
    current = level_zero
    for section_no in range(1, section_count + 1):
        group_size = 1 << section_no
        half_size = group_size >> 1
        position = band_pos % group_size
        partner = from_partner(current, "band", section_no - 1)
        upper_side = position >= half_size
        lower_half = jnp.where(upper_side, partner, current)
        upper_half = jnp.where(upper_side, current, partner)
        node_no = band_pos // group_size
        section_slope = pick_entry(
            merge_slope, node_no * (2 * group_size) + group_size - 1
        ).reshape(1)
        out_index = position * block_rows + lax.iota(jnp.int32, block_rows)
        current = merge_nodes(lower_half, upper_half, out_index, section_slope, bins_index, length)
    spectra = current[:, 0]
    bordered = extended(spectra, (("freq", 2),), REACH)
    width = 2 * LANES
    span = lax.iota(jnp.int32, width)
    matches = tap_offset[:, :, None] + REACH == span[None, None, :]
    profile = jnp.sum(jnp.where(matches, tap_weight[:, :, None], 0.0), axis=1)
    cells = jnp.pad(bordered, ((0, 0), (0, 0), (0, LANES - 2 * REACH)))
    return template_search(profile, cells.reshape(2 * block_rows, bins_dev + LANES), bins_dev)


def solution(mesh):
    placed = (P("band", "freq"), P("band", None), P(), P(), P())
    return jax.shard_map(
        per_device, mesh=mesh, in_specs=placed, out_specs=P("band", "freq"), check_vma=False
    )
```

```python
import functools
import math

import jax
import jax.numpy as jnp
import numpy as np
from jax import lax
from jax.experimental import pallas as pl
from jax.experimental.pallas import tpu as pltpu
from jax.sharding import PartitionSpec as P

REACH = 32
DELAY_BOUND = 4096
LANES = 128
GROUP = 8


two_pi = 2.0 * math.pi


def from_partner(value, axis, stride):
    return lax.ppermute(value, axis, [(i, i ^ 1 << stride) for i in range(lax.axis_size(axis))])


def extended(cells, sides, width):
    for axis, dim in sides:
        count = lax.axis_size(axis)
        ends = count - 1
        head = lax.slice_in_dim(cells, 0, width, axis=dim)
        tail = lax.slice_in_dim(cells, cells.shape[dim] - width, cells.shape[dim], axis=dim)
        cells = jnp.concatenate(
            [
                lax.ppermute(tail, axis, [(i, (i + 1) % count) for i in range(ends)]),
                cells,
                lax.ppermute(head, axis, [((i + 1) % count, i) for i in range(ends)]),
            ],
            axis=dim,
        )
    return cells


def turning(count, modulus):
    angle = (count % modulus).astype(jnp.float32) * (two_pi / modulus)
    return (jnp.cos(angle), jnp.sin(angle))


def rotate(real, imag, cosine, sine_part):
    return (real * cosine + imag * sine_part, imag * cosine - real * sine_part)


def merge_nodes(lower_half, upper_half, out_index, slopes, bins_index, modulus):
    shift = out_index[None, :] * slopes[:, None] // 16 % modulus
    cosine, sine_part = turning(shift[:, :, None] * bins_index[None, None, :], modulus)
    up_re, up_im = rotate(upper_half[0], upper_half[1], cosine, sine_part)
    return jnp.stack([lower_half[0] + up_re, lower_half[1] + up_im]) * (1.0 / math.sqrt(2.0))


def pick_entry(table, index):
    return jnp.sum(jnp.where(lax.iota(jnp.int32, table.shape[0]) == index, table, 0))


def shift_sum_kernel(has_base, delay_ref, series_ref, *refs):
    base_ref = refs[0] if has_base else None
    out_ref, rows_ref, window_ref = refs[has_base:]
    step = pl.program_id(0)
    parts, _, part_len = series_ref.shape
    outer = part_len // LANES
    count = parts * outer
    turns = DELAY_BOUND // LANES
    for part in range(parts):
        for block in range(outer):
            rows_ref[pl.ds((part * outer + block) * GROUP, GROUP), :] = series_ref[
                part, :, block * LANES : (block + 1) * LANES
            ]

    for chan in range(GROUP):
        grid = rows_ref[pl.ds(chan, count, stride=GROUP), :].T
        for turn in range(turns + 1):
            shift = (turns - turn) % count
            window_ref[chan, turn * LANES : (turn + 1) * LANES, :] = (
                pltpu.roll(grid, shift, 1) if shift else grid
            )

    @pl.when(step == 0)
    def _():
        out_ref[...] = base_ref[...] if has_base else jnp.zeros_like(out_ref)

    def one_delay(delay_no, carry):
        total = out_ref[delay_no]
        for chan in range(GROUP):
            start = DELAY_BOUND - delay_ref[step * GROUP + chan, delay_no]
            total = total + window_ref[chan, pl.ds(start, LANES), :]
        out_ref[delay_no] = total
        return carry

    lax.fori_loop(0, out_ref.shape[0], one_delay, 0)


def shift_sum(delays, series, base):
    parts, chan_count, part_len = series.shape
    delay_count = delays.shape[1]
    count = parts * part_len // LANES
    has_base = base is not None
    block = pl.BlockSpec((delay_count, LANES, count), lambda i, _: (0, 0, 0))
    return pl.pallas_call(
        functools.partial(shift_sum_kernel, int(has_base)),
        out_shape=jax.ShapeDtypeStruct((delay_count, LANES, count), jnp.float32),
        grid_spec=pltpu.PrefetchScalarGridSpec(
            num_scalar_prefetch=1,
            grid=(chan_count // GROUP,),
            in_specs=[pl.BlockSpec((parts, GROUP, part_len), lambda i, _: (0, i, 0))]
            + [block] * has_base,
            out_specs=block,
            scratch_shapes=[
                pltpu.VMEM((count * GROUP, LANES), jnp.float32),
                pltpu.VMEM((GROUP, DELAY_BOUND + LANES, count), jnp.float32),
            ],
        ),
        input_output_aliases={2: 0} if has_base else {},
        cost_estimate=pl.CostEstimate(
            flops=1000 * chan_count * parts * part_len * delay_count // 8,
            bytes_accessed=4 * (series.size + delay_count * LANES * count),
            transcendentals=0,
        ),
        compiler_params=pltpu.CompilerParams(vmem_limit_bytes=48 << 20),
        name="shift_sum",
    )(delays, series, *([base] if has_base else []))


def chunk_sizes(group_count):
    if group_count < 8:
        return [1] * group_count if group_count <= 4 else [group_count - 3, 1, 1, 1]
    last = group_count // 8
    return [group_count - 5 * last, 2 * last, 2 * last, last]


def reduce_halving(value, pos, bits):
    left = sorted(bits, reverse=True)
    for bit in bits:
        dim = left.index(bit)
        mine = pos >> bit & 1
        kept = lax.dynamic_index_in_dim(value, mine, dim, keepdims=False)
        sent = lax.dynamic_index_in_dim(value, 1 - mine, dim, keepdims=False)
        value = kept + from_partner(sent, "freq", bit)
        left.remove(bit)
    return value


def split_halves(value):
    coarse = value.astype(jnp.bfloat16)
    fine = (value - coarse.astype(jnp.float32)).astype(jnp.bfloat16)
    return coarse, fine


def table_halves(table, dim):
    coarse = table.astype(jnp.bfloat16)
    fine = (table - coarse.astype(np.float64)).astype(jnp.bfloat16)
    return jnp.asarray(np.concatenate([coarse, coarse, fine], axis=dim))


def dft_kernel(first_ref, twist_cos_ref, twist_sin_ref, second_ref, series_ref, out_ref):
    count = series_ref.shape[2]
    coarse, fine = split_halves(series_ref[0])
    part_out = jnp.dot(
        jnp.concatenate([coarse, fine, coarse], axis=1),
        first_ref[...],
        preferred_element_type=jnp.float32,
    )
    real, imag = rotate(
        part_out[:, :count], part_out[:, count:], twist_cos_ref[...], twist_sin_ref[...]
    )
    coarse, fine = split_halves(jnp.concatenate([real, imag], axis=0))
    spectrum = jnp.dot(
        second_ref[...],
        jnp.concatenate([coarse, fine, coarse], axis=0),
        preferred_element_type=jnp.float32,
    )
    slabs, _, _, rows, _ = out_ref.shape
    half = slabs * rows
    for slab in range(slabs):
        out_ref[slab, 0, 0] = spectrum[slab * rows : (slab + 1) * rows]
        out_ref[slab, 1, 0] = spectrum[half + slab * rows : half + (slab + 1) * rows]


def dft(series, slabs, scale):
    row_count, inner, outer = series.shape
    length = inner * outer
    kept = inner // 2
    rows = kept // slabs
    index = np.arange(outer)
    angle = (index[:, None] * index[None, :] % outer) * (two_pi / outer)
    first = np.concatenate([np.cos(angle), -np.sin(angle)], axis=1)
    angle = (np.arange(inner)[:, None] * index[None, :]) * (two_pi / length)
    twist_cos, twist_sin = np.cos(angle), np.sin(angle)
    angle = (np.arange(kept)[:, None] * np.arange(inner)[None, :] % inner) * (two_pi / inner)
    cosine, sine_part = np.cos(angle) * scale, np.sin(angle) * scale
    second = np.block([[cosine, sine_part], [-sine_part, cosine]])
    first, second = table_halves(first, 0), table_halves(second, 1)
    tables = [first, jnp.asarray(twist_cos, jnp.float32), jnp.asarray(twist_sin, jnp.float32), second]
    whole = [pl.BlockSpec(t.shape, lambda i: (0, 0)) for t in tables]
    return pl.pallas_call(
        dft_kernel,
        out_shape=jax.ShapeDtypeStruct((slabs, 2, row_count, rows, outer), jnp.float32),
        grid=(row_count,),
        in_specs=whole
        + [pl.BlockSpec((1, inner, outer), lambda i: (i, 0, 0))],
        out_specs=pl.BlockSpec((slabs, 2, 1, rows, outer), lambda i: (0, 0, i, 0, 0)),
        name="dft",
    )(*tables, series)


def template_kernel(profile_ref, left_ref, right_ref, out_ref, bank_ref):
    template_count, width = profile_ref.shape

    @pl.when(pl.program_id(0) == 0)
    def _():
        def one_template(template_no, carry):
            row = jnp.broadcast_to(profile_ref[pl.ds(template_no, 1), :], (LANES, width))
            coarse, fine = split_halves(pltpu.roll(row, 0, 1, stride=1, stride_axis=0))
            where = pl.ds(pl.multiple_of(template_no * LANES, LANES), LANES)
            bank_ref[where, :] = jnp.concatenate([coarse, coarse, fine], axis=1)
            return carry

        lax.fori_loop(0, template_count, one_template, 0)

    coarse, fine = split_halves(jnp.concatenate([left_ref[...], right_ref[...]], axis=1))
    cells = jnp.concatenate([coarse, fine, coarse], axis=1)
    rows = out_ref.shape[0]
    best = jnp.zeros_like(out_ref)
    for pair in range(template_count // 2):
        corr = lax.dot_general(
            cells,
            bank_ref[pair * 2 * LANES : (pair + 1) * 2 * LANES, :],
            (((1,), (1,)), ((), ())),
            preferred_element_type=jnp.float32,
        )
        power = corr[:rows] * corr[:rows] + corr[rows:] * corr[rows:]
        best = jnp.maximum(best, jnp.maximum(power[:, :LANES], power[:, LANES:]))
    out_ref[...] = best


def template_search(profile, cells, bins_dev):
    rows = cells.shape[0] // 2
    template_count, width = profile.shape
    return pl.pallas_call(
        template_kernel,
        out_shape=jax.ShapeDtypeStruct((rows, bins_dev), jnp.float32),
        grid=(bins_dev // LANES,),
        in_specs=[
            pl.BlockSpec((template_count, width), lambda i: (0, 0)),
            pl.BlockSpec((2 * rows, LANES), lambda i: (0, i)),
            pl.BlockSpec((2 * rows, LANES), lambda i: (0, i + 1)),
        ],
        out_specs=pl.BlockSpec((rows, LANES), lambda i: (0, i)),
        scratch_shapes=[pltpu.VMEM((template_count * LANES, 3 * width), jnp.bfloat16)],
        compiler_params=pltpu.CompilerParams(vmem_limit_bytes=48 << 20),
        name="template_search",
    )(profile, cells, cells)


def per_device(samples, channel_delay, merge_slope, tap_offset, tap_weight):
    freq_count = lax.axis_size("freq")
    band_count = lax.axis_size("band")
    band_pos = lax.axis_index("band")
    freq_pos = lax.axis_index("freq")
    chan_dev, samp_dev = samples.shape
    length = samp_dev * freq_count
    bins_dev = length // 2 // freq_count
    delays_sub = channel_delay.shape[1]
    block_rows = 2 * delays_sub
    per_sub = chan_dev // 2
    chan_own = chan_dev // freq_count
    share = per_sub // chan_own
    bins_index = freq_pos * bins_dev + lax.iota(jnp.int32, bins_dev)

    own_delay = lax.dynamic_slice_in_dim(channel_delay, freq_pos * chan_own, chan_own, axis=0)
    by_owner = samples.reshape(freq_count, chan_own, samp_dev)
    start, waiting, previous, partial = 0, None, None, None
    for groups in chunk_sizes(chan_own // GROUP):
        end = start + groups * GROUP
        chunk = by_owner[:, start:end]
        if previous is not None:
            chunk, previous = lax.optimization_barrier((chunk, previous))
        series = lax.all_to_all(chunk, "freq", split_axis=0, concat_axis=0, tiled=True)
        if waiting is not None:
            previous = partial = shift_sum(*waiting, partial)
        waiting = own_delay[start:end], series
        start = end
    partial = shift_sum(*waiting, partial)

    inner, outer = partial.shape[1:]
    bits = list(range(share.bit_length() - 1))
    rows = delays_sub // (2 * share)
    streams = partial.reshape([2] + [2] * len(bits) + [rows, inner, outer])
    owned = jnp.concatenate(
        [
            reduce_halving(streams[0], freq_pos, bits),
            reduce_halving(streams[1], freq_pos, bits[::-1]),
        ]
    )
    slabs = dft(owned, freq_count, 1.0 / math.sqrt(length * per_sub))
    slabs = lax.all_to_all(slabs, "freq", split_axis=0, concat_axis=0, tiled=True)
    subband_sums = (
        slabs.reshape(2, share, 2, 2, rows, bins_dev)
        .transpose(2, 0, 3, 1, 4, 5)
        .reshape(2, 2, delays_sub, bins_dev)
    )
    lower_half = jnp.concatenate([subband_sums[:, 0:1], subband_sums[:, 0:1]], axis=2)
    upper_half = jnp.concatenate([subband_sums[:, 1:2], subband_sums[:, 1:2]], axis=2)
    first_slope = pick_entry(merge_slope, 2 * band_pos).reshape(1)
    level_zero = merge_nodes(
        lower_half, upper_half, lax.iota(jnp.int32, block_rows), first_slope, bins_index, length
    )
    section_count = band_count.bit_length() - 1
    current = level_zero
    for section_no in range(1, section_count + 1):
        group_size = 1 << section_no
        half_size = group_size >> 1
        position = band_pos % group_size
        partner = from_partner(current, "band", section_no - 1)
        upper_side = position >= half_size
        lower_half = jnp.where(upper_side, partner, current)
        upper_half = jnp.where(upper_side, current, partner)
        node_no = band_pos // group_size
        section_slope = pick_entry(
            merge_slope, node_no * (2 * group_size) + group_size - 1
        ).reshape(1)
        out_index = position * block_rows + lax.iota(jnp.int32, block_rows)
        current = merge_nodes(lower_half, upper_half, out_index, section_slope, bins_index, length)
    spectra = current[:, 0]
    bordered = extended(spectra, (("freq", 2),), REACH)
    width = 2 * LANES
    span = lax.iota(jnp.int32, width)
    matches = tap_offset[:, :, None] + REACH == span[None, None, :]
    profile = jnp.sum(jnp.where(matches, tap_weight[:, :, None], 0.0), axis=1)
    cells = jnp.pad(bordered, ((0, 0), (0, 0), (0, LANES - 2 * REACH)))
    return template_search(profile, cells.reshape(2 * block_rows, bins_dev + LANES), bins_dev)


def solution(mesh):
    placed = (P("band", "freq"), P("band", None), P(), P(), P())
    return jax.shard_map(
        per_device, mesh=mesh, in_specs=placed, out_specs=P("band", "freq"), check_vma=False
    )
```

```python
import functools
import math

import jax
import jax.numpy as jnp
import numpy as np
from jax import lax
from jax.experimental import pallas as pl
from jax.experimental.pallas import tpu as pltpu
from jax.sharding import PartitionSpec as P

REACH = 32
DELAY_BOUND = 4096
LANES = 128
GROUP = 8


two_pi = 2.0 * math.pi


def from_partner(value, axis, stride):
    return lax.ppermute(value, axis, [(i, i ^ 1 << stride) for i in range(lax.axis_size(axis))])


def turning(count, modulus):
    angle = (count % modulus).astype(jnp.float32) * (two_pi / modulus)
    return (jnp.cos(angle), jnp.sin(angle))


def rotate(real, imag, cosine, sine_part):
    return (real * cosine + imag * sine_part, imag * cosine - real * sine_part)


def merge_nodes(lower_half, upper_half, out_index, slope, bins_index, modulus):
    shift = out_index * slope // 16 % modulus
    cosine, sine_part = turning(shift[None, :, None] * bins_index[:, None, :], modulus)
    up_re, up_im = rotate(upper_half[0], upper_half[1], cosine, sine_part)
    return jnp.stack([lower_half[0] + up_re, lower_half[1] + up_im]) * (1.0 / math.sqrt(2.0))


def pick_entry(table, index):
    return jnp.sum(jnp.where(lax.iota(jnp.int32, table.shape[0]) == index, table, 0))


def shift_sum_kernel(has_base, delay_ref, series_ref, *refs):
    base_ref = refs[0] if has_base else None
    out_ref, rows_ref, window_ref = refs[has_base:]
    step = pl.program_id(0)
    parts, _, part_len = series_ref.shape
    outer = part_len // LANES
    count = parts * outer
    turns = DELAY_BOUND // LANES
    for part in range(parts):
        for block in range(outer):
            rows_ref[pl.ds((part * outer + block) * GROUP, GROUP), :] = series_ref[
                part, :, block * LANES : (block + 1) * LANES
            ]

    for chan in range(GROUP):
        grid = rows_ref[pl.ds(chan, count, stride=GROUP), :].T
        for turn in range(turns + 1):
            shift = (turns - turn) % count
            window_ref[chan, turn * LANES : (turn + 1) * LANES, :] = (
                pltpu.roll(grid, shift, 1) if shift else grid
            )

    @pl.when(step == 0)
    def _():
        out_ref[...] = base_ref[...] if has_base else jnp.zeros_like(out_ref)

    def one_delay(delay_no, carry):
        total = out_ref[delay_no]
        for chan in range(GROUP):
            start = DELAY_BOUND - delay_ref[step * GROUP + chan, delay_no]
            total = total + window_ref[chan, pl.ds(start, LANES), :]
        out_ref[delay_no] = total
        return carry

    lax.fori_loop(0, out_ref.shape[0], one_delay, 0)


def shift_sum(delays, series, base):
    parts, chan_count, part_len = series.shape
    delay_count = delays.shape[1]
    count = parts * part_len // LANES
    has_base = base is not None
    block = pl.BlockSpec((delay_count, LANES, count), lambda i, _: (0, 0, 0))
    return pl.pallas_call(
        functools.partial(shift_sum_kernel, int(has_base)),
        out_shape=jax.ShapeDtypeStruct((delay_count, LANES, count), jnp.float32),
        grid_spec=pltpu.PrefetchScalarGridSpec(
            num_scalar_prefetch=1,
            grid=(chan_count // GROUP,),
            in_specs=[pl.BlockSpec((parts, GROUP, part_len), lambda i, _: (0, i, 0))]
            + [block] * has_base,
            out_specs=block,
            scratch_shapes=[
                pltpu.VMEM((count * GROUP, LANES), jnp.float32),
                pltpu.VMEM((GROUP, DELAY_BOUND + LANES, count), jnp.float32),
            ],
        ),
        input_output_aliases={2: 0} if has_base else {},
        cost_estimate=pl.CostEstimate(
            flops=1000 * chan_count * parts * part_len * delay_count // 8,
            bytes_accessed=4 * (series.size + delay_count * LANES * count),
            transcendentals=0,
        ),
        compiler_params=pltpu.CompilerParams(vmem_limit_bytes=48 << 20),
        name="shift_sum",
    )(delays, series, *([base] if has_base else []))


def chunk_sizes(group_count):
    if group_count < 8:
        return [1] * group_count
    last = group_count // 8
    return [group_count - 4 * last, 3 * last, last]


def reduce_halving(value, pos, bits):
    left = sorted(bits, reverse=True)
    for bit in bits:
        dim = left.index(bit)
        mine = pos >> bit & 1
        kept = lax.dynamic_index_in_dim(value, mine, dim, keepdims=False)
        sent = lax.dynamic_index_in_dim(value, 1 - mine, dim, keepdims=False)
        value = kept + from_partner(sent, "freq", bit)
        left.remove(bit)
    return value


def split_halves(value):
    coarse = value.astype(jnp.bfloat16)
    fine = (value - coarse.astype(jnp.float32)).astype(jnp.bfloat16)
    return coarse, fine


def table_halves(table, dim):
    coarse = table.astype(jnp.bfloat16)
    fine = (table - coarse.astype(np.float64)).astype(jnp.bfloat16)
    return jnp.asarray(np.concatenate([coarse, coarse, fine], axis=dim))


def dft_kernel(first_ref, twist_cos_ref, twist_sin_ref, second_ref, series_ref, out_ref):
    rows, inner, outer = series_ref.shape
    coarse, fine = split_halves(series_ref[...].reshape(rows * inner, outer))
    part_out = jnp.dot(
        jnp.concatenate([coarse, fine, coarse], axis=1),
        first_ref[...],
        preferred_element_type=jnp.float32,
    )
    turned = []
    for row in range(rows):
        part = part_out[row * inner : (row + 1) * inner]
        real, imag = rotate(
            part[:, :outer], part[:, outer:], twist_cos_ref[...], twist_sin_ref[...]
        )
        turned.append(jnp.concatenate([real, imag], axis=0))
    coarse, fine = split_halves(jnp.concatenate(turned, axis=1))
    spectrum = jnp.dot(
        second_ref[...],
        jnp.concatenate([coarse, fine, coarse], axis=0),
        preferred_element_type=jnp.float32,
    )
    slabs, _, tiles, _, _ = out_ref.shape
    tiles -= 1
    half = slabs * tiles
    lane = lax.broadcasted_iota(jnp.int32, (1, outer), 1)
    none = jnp.zeros((1, outer), jnp.float32)
    for row in range(rows):
        for part in range(2):
            bins = spectrum[part * half : (part + 1) * half, row * outer : (row + 1) * outer]
            for slab in range(slabs):
                low, high = slab * tiles, (slab + 1) * tiles
                out_ref[slab, part, 0:tiles, row, :] = bins[low:high]
                after = bins[high : high + 1] if high < half else none
                before = bins[low - 1 : low] if low else none
                out_ref[slab, part, tiles, row : row + 1, :] = jnp.where(
                    lane < outer // 2, after, before
                )


def dft(series, slabs, scale):
    row_count, inner, outer = series.shape
    length = inner * outer
    kept = inner // 2
    tiles = kept // slabs + 1
    rows = math.gcd(row_count, 8)
    index = np.arange(outer)
    angle = (index[:, None] * index[None, :] % outer) * (two_pi / outer)
    first = np.concatenate([np.cos(angle), -np.sin(angle)], axis=1)
    angle = (np.arange(inner)[:, None] * index[None, :]) * (two_pi / length)
    twist_cos, twist_sin = np.cos(angle), np.sin(angle)
    angle = (np.arange(kept)[:, None] * np.arange(inner)[None, :] % inner) * (two_pi / inner)
    cosine, sine_part = np.cos(angle) * scale, np.sin(angle) * scale
    second = np.block([[cosine, sine_part], [-sine_part, cosine]])
    first, second = table_halves(first, 0), table_halves(second, 1)
    tables = [first, jnp.asarray(twist_cos, jnp.float32), jnp.asarray(twist_sin, jnp.float32), second]
    whole = [pl.BlockSpec(t.shape, lambda i: (0, 0)) for t in tables]
    return pl.pallas_call(
        dft_kernel,
        out_shape=jax.ShapeDtypeStruct((slabs, 2, tiles, row_count, outer), jnp.float32),
        grid=(row_count // rows,),
        in_specs=whole + [pl.BlockSpec((rows, inner, outer), lambda i: (i, 0, 0))],
        out_specs=pl.BlockSpec((slabs, 2, tiles, rows, outer), lambda i: (0, 0, 0, i, 0)),
        name="dft",
    )(*tables, series)


def template_kernel(first_step, profile_ref, before_ref, tile_ref, after_ref, *refs):
    out_ref, bank_ref = refs[-2:]
    template_count, width = profile_ref.shape

    @pl.when(pl.program_id(0) == 0)
    def _():
        def one_template(template_no, carry):
            row = jnp.broadcast_to(profile_ref[pl.ds(template_no, 1), :], (LANES, width))
            coarse, fine = split_halves(pltpu.roll(row, 0, 1, stride=1, stride_axis=0))
            where = pl.ds(pl.multiple_of(template_no * LANES, LANES), LANES)
            bank_ref[where, :] = jnp.concatenate([coarse, coarse, fine], axis=1)
            return carry

        lax.fori_loop(0, template_count, one_template, 0)

    rows = out_ref.shape[0]
    lane = lax.broadcasted_iota(jnp.int32, (2 * rows, LANES), 1)
    tile, after, before = (
        ref[...].reshape(2 * rows, LANES) for ref in (tile_ref, after_ref, before_ref)
    )
    border = jnp.where(lane < LANES // 2, after, before)
    coarse, fine = split_halves(jnp.concatenate([tile, border], axis=1))
    cells = jnp.concatenate([coarse, fine, coarse], axis=1)
    best = jnp.zeros_like(out_ref)
    for pair in range(template_count // 2):
        corr = lax.dot_general(
            cells,
            bank_ref[pair * 2 * LANES : (pair + 1) * 2 * LANES, :],
            (((1,), (1,)), ((), ())),
            preferred_element_type=jnp.float32,
        )
        power = corr[:rows] * corr[:rows] + corr[rows:] * corr[rows:]
        best = jnp.maximum(best, jnp.maximum(power[:, :LANES], power[:, LANES:]))
    out_ref[...] = best


def template_search(profile, cells, borders, tiles, first, filled):
    run, rows = cells.shape[1:3]
    template_count, width = profile.shape
    shape = (2, 1, rows, LANES)
    cells = jnp.concatenate([borders[:, :1], cells, borders[:, 1:]], axis=1)
    specs = [pl.BlockSpec((template_count, width), lambda i: (0, 0))]
    for step in range(3):
        specs.append(pl.BlockSpec(shape, lambda i, step=step: (0, i + step, 0, 0)))
    operands = [profile, cells, cells, cells]
    if filled is not None:
        specs.append(pl.BlockSpec(memory_space=pl.ANY))
        operands.append(filled)
    return pl.pallas_call(
        functools.partial(template_kernel, first),
        out_shape=jax.ShapeDtypeStruct((rows, tiles * LANES), jnp.float32),
        grid=(run,),
        in_specs=specs,
        out_specs=pl.BlockSpec((rows, LANES), lambda i: (0, i + first)),
        scratch_shapes=[pltpu.VMEM((template_count * LANES, 3 * width), jnp.bfloat16)],
        input_output_aliases={} if filled is None else {4: 0},
        cost_estimate=pl.CostEstimate(
            flops=1000 * run * rows * template_count * width * LANES,
            bytes_accessed=4 * cells.size,
            transcendentals=0,
        ),
        compiler_params=pltpu.CompilerParams(vmem_limit_bytes=48 << 20),
        name="template_search",
    )(*operands)


def per_device(samples, channel_delay, merge_slope, tap_offset, tap_weight):
    freq_count = lax.axis_size("freq")
    band_count = lax.axis_size("band")
    band_pos = lax.axis_index("band")
    freq_pos = lax.axis_index("freq")
    chan_dev, samp_dev = samples.shape
    length = samp_dev * freq_count
    bins_dev = length // 2 // freq_count
    delays_sub = channel_delay.shape[1]
    block_rows = 2 * delays_sub
    per_sub = chan_dev // 2
    chan_own = chan_dev // freq_count
    share = per_sub // chan_own
    own_delay = lax.dynamic_slice_in_dim(channel_delay, freq_pos * chan_own, chan_own, axis=0)
    by_owner = samples.reshape(freq_count, chan_own, samp_dev)
    start, waiting, previous, partial = 0, None, None, None
    for groups in chunk_sizes(chan_own // GROUP):
        end = start + groups * GROUP
        chunk = by_owner[:, start:end]
        if previous is not None:
            chunk, previous = lax.optimization_barrier((chunk, previous))
        series = lax.all_to_all(chunk, "freq", split_axis=0, concat_axis=0, tiled=True)
        if waiting is not None:
            previous = partial = shift_sum(*waiting, partial)
        waiting = own_delay[start:end], series
        start = end
    partial = shift_sum(*waiting, partial)

    inner, outer = partial.shape[1:]
    bits = list(range(share.bit_length() - 1))
    rows = delays_sub // (2 * share)
    streams = partial.reshape([2] + [2] * len(bits) + [rows, inner, outer])
    owned = jnp.concatenate(
        [
            reduce_halving(streams[0], freq_pos, bits),
            reduce_halving(streams[1], freq_pos, bits[::-1]),
        ]
    )
    slabs = dft(owned, freq_count, 1.0 / math.sqrt(length * per_sub))
    slabs = lax.all_to_all(slabs, "freq", split_axis=0, concat_axis=0, tiled=True)
    tiles = bins_dev // LANES
    spot = lax.iota(jnp.int32, bins_dev + LANES)
    spot = jnp.where(spot < bins_dev + LANES // 2, spot, spot - bins_dev - LANES)
    bins_index = (freq_pos * bins_dev + spot).reshape(tiles + 1, LANES)
    subband_sums = (
        slabs.reshape(2, share, 2, tiles + 1, 2, rows, LANES)
        .transpose(2, 0, 3, 4, 1, 5, 6)
        .reshape(2, 2, tiles + 1, delays_sub, LANES)
    )
    first_slope = pick_entry(merge_slope, 2 * band_pos)
    current = merge_nodes(
        jnp.concatenate([subband_sums[:, 0]] * 2, axis=2),
        jnp.concatenate([subband_sums[:, 1]] * 2, axis=2),
        lax.iota(jnp.int32, block_rows), first_slope, bins_index, length,
    )

    def section(current, partner, section_no, bins_index):
        group_size = 1 << section_no
        position = band_pos % group_size
        upper_side = position >= group_size >> 1
        lower_half = jnp.where(upper_side, partner, current)
        upper_half = jnp.where(upper_side, current, partner)
        node_no = band_pos // group_size
        slope = pick_entry(merge_slope, node_no * (2 * group_size) + group_size - 1)
        out_index = position * block_rows + lax.iota(jnp.int32, block_rows)
        return merge_nodes(lower_half, upper_half, out_index, slope, bins_index, length)

    section_count = band_count.bit_length() - 1
    for section_no in range(1, section_count):
        partner = from_partner(current, "band", section_no - 1)
        current = section(current, partner, section_no, bins_index)

    width = 2 * LANES
    span = lax.iota(jnp.int32, width)
    matches = (tap_offset % width)[:, :, None] == span[None, None, :]
    profile = jnp.sum(jnp.where(matches, tap_weight[:, :, None], 0.0), axis=1)

    cut = tiles // 2
    early = jnp.concatenate([current[:, tiles:], current[:, : cut + 1]], axis=1)
    early_bins = jnp.concatenate([bins_index[tiles:], bins_index[: cut + 1]])
    late, late_bins = current[:, cut + 1 : tiles], bins_index[cut + 1 : tiles]
    if section_count:
        early_partner = from_partner(early, "band", section_count - 1)
        early_partner, late = lax.optimization_barrier((early_partner, late))
        late_partner = from_partner(late, "band", section_count - 1)
        early = section(early, early_partner, section_count, early_bins)
    power = template_search(
        profile, early[:, 1 : cut + 1], early[:, :: cut + 1], tiles, 0, None
    )
    if section_count:
        late, power = lax.optimization_barrier((late, power))
        late = section(late, late_partner, section_count, late_bins)
    return template_search(
        profile,
        jnp.concatenate([early[:, cut + 1 :], late], axis=1),
        jnp.concatenate([early[:, cut : cut + 1], early[:, :1]], axis=1),
        tiles, cut, power,
    )


def solution(mesh):
    placed = (P("band", "freq"), P("band", None), P(), P(), P())
    return jax.shard_map(
        per_device, mesh=mesh, in_specs=placed, out_specs=P("band", "freq"), check_vma=False
    )
```
